128 devices in a mesh: dp: 32 (over y, x, core), fsdp: 4 (over z).
Axes of the slice: x: 4, y: 4, z: 4, core: 2. Of those that a mesh axis runs over, the one named last changes fastest.
Arguments:
- memory: bfloat16 [16384, 4096], P('dp'), may hold values from -6 to 6
- key_weight: bfloat16 [4096, 2048], P('dp', 'fsdp'), may hold values from -0.09375 to 0.09375
- value_weight: bfloat16 [4096, 2048], P('dp', 'fsdp'), may hold values from -0.09375 to 0.09375
- query: bfloat16 [16384, 2048], P('dp', 'fsdp')
- grad_context: bfloat16 [16384, 2048], P('dp', 'fsdp')
- target_segment: int32 [32, 512], P('dp'), may hold values from 0 to 31, never falling along the last dimension, each value on 1 to 32 neighbouring positions
- memory_segment: int32 [32, 512], P('dp'), may hold values from 0 to 31, never falling along the last dimension, each value on 1 to 128 neighbouring positions
- example_pack: int32 [32, 32], replicated, may hold values from 0 to 31, as said below
- example_slot: int32 [32, 32], replicated, may hold values from 0 to 31, as said below
Outputs:
- context: bfloat16 [16384, 2048], P('dp', 'fsdp')
- grad_query: bfloat16 [16384, 2048], P('dp', 'fsdp')
- grad_key_weight: float32 [4096, 2048], P('dp', 'fsdp')
- grad_value_weight: float32 [4096, 2048], P('dp', 'fsdp')
- grad_memory: bfloat16 [16384, 4096], P(('dp', 'fsdp'))
The draws below stay inside these ranges and needn't reach their ends.
Inputs may be any that keep to these rules, and one draw needn't show every extreme that they name: `target_segment`: rows of each target pack are ordered by example; every one of the 32 examples has 1 to 32 decoder rows, and some example has exactly 32. `memory_segment`: rows of each input pack are ordered by segment; every one of the 32 segments has 1 to 128 memory rows, and some segment has exactly 128. `example_pack`: the 32 examples of one target pack have their memory in 32 different input packs, and every input pack holds the memory of exactly 32 examples. `example_slot`: the examples whose memory lies in one input pack carry the segment numbers 0 to 31 of that pack, each once.
All inputs are finite; a program needn't handle non-finite values.
Results may differ from the reference program's by a relative error of at most 0.017.
Values may be sent and summed in bfloat16 or wider, within the bound.
No kernel may reach another device: no remote copies, remote signals or barrier semaphores. Data moves between devices by JAX's collectives and lax.ppermute only.
A program may use at most 128 MiB of HBM per device.

```python
import math
import jax
import jax.numpy as jnp
import numpy as np
from jax import lax

D = 4096
H = 8
HD = 256
TGT = 512
EXT = 32
M_DEV = 512
MAXM = 128
QP = 32
MEM_ROWS = 16384
TGT_ROWS = 16384
N_DP = 32


def draw_query(key, part):
    base = jnp.clip(jax.random.normal(jax.random.fold_in(key, 1), (TGT_ROWS, H * HD), jnp.float32), -6.0, 6.0)
    return base.astype(jnp.bfloat16)


def draw_grad_context(key, part):
    base = jnp.clip(jax.random.normal(jax.random.fold_in(key, 21), (TGT_ROWS, H * HD), jnp.float32), -6.0, 6.0)
    return base.astype(jnp.bfloat16)


def route_tables(key):
    inner_key = jax.random.fold_in(key, 7)
    shuffle_out = jax.random.permutation(jax.random.fold_in(inner_key, 1), N_DP).astype(jnp.int32)
    shuffle_in = jax.random.permutation(jax.random.fold_in(inner_key, 2), N_DP).astype(jnp.int32)
    offsets = jax.random.permutation(jax.random.fold_in(inner_key, 3), N_DP).astype(jnp.int32)[:EXT]
    rotation = jax.random.randint(jax.random.fold_in(inner_key, 4), (N_DP,), 0, EXT).astype(jnp.int32)
    target_ids = jnp.arange(N_DP, dtype=jnp.int32)[:, None]
    inner = (shuffle_in[target_ids] + offsets[None, :]) % N_DP
    packs = shuffle_out[inner]
    example_ids = jnp.arange(EXT, dtype=jnp.int32)[None, :]
    slots = (example_ids + rotation[packs]) % EXT
    return (packs.astype(jnp.int32), slots.astype(jnp.int32))


def draw_example_pack(key, part):
    return route_tables(key)[0]


def draw_example_slot(key, part):
    return route_tables(key)[1]


def spiked(drawn, key, source, target, shards_of, factor):
    owner, partner = [(jnp.arange(drawn.shape[axis_at]) // (drawn.shape[axis_at] // shards_of)).reshape([-1 if axis == axis_at else 1 for axis in range(drawn.ndim)]) for axis_at in (source, target)]
    chosen = jax.random.permutation(key, shards_of)[partner]
    strong = (owner == chosen) | (owner == (partner + shards_of // 2) % shards_of)
    return jnp.where(strong, factor * drawn, drawn)


def block_levels(key, shape, cuts, least, largest):
    gain, own = 1.0, jax.random.fold_in(key, 6)
    for dim, shards_of in cuts:
        heights = jnp.exp(jax.random.uniform(jax.random.fold_in(own, dim), (shards_of,), jnp.float32, least / len(cuts), largest / len(cuts)))
        gain = gain * jnp.repeat(heights, shape[dim] // shards_of).reshape([-1 if axis == dim else 1 for axis in range(len(shape))])
    return gain


def profile(count, total, reach, skew):
    loads = [(1 << 20) // math.isqrt(standing ** skew) + 1 for standing in range(2, count + 1)]
    spare, given = total - reach - (count - 1), [1] * (count - 1)
    while spare > 0:
        movable = [i for i in range(count - 1) if given[i] < reach]
        mass, budget = sum([loads[i] for i in movable]), spare
        for i in movable:
            extra = min(reach - given[i], max(1, budget * loads[i] // mass), spare)
            given[i] = given[i] + extra
            spare = spare - extra
    return np.array([reach] + given)


def ragged(key, amount, total, bound, lean):
    if amount == 2:
        one = jax.random.randint(key, (), max(1, total - bound), min(bound, total - 1) + 1)
        return jnp.stack([one, total - one])
    tallies = jnp.asarray(profile(amount, total, bound, lean), jnp.int32)
    couples = (amount - 1) // 2
    source_of, receiver = tallies[1:1 + 2 * couples:2], tallies[2:2 + 2 * couples:2]
    room = jnp.minimum(source_of - 1, bound - receiver)
    passed = jax.random.randint(jax.random.fold_in(key, 1), (couples,), 0, 1 << 20) % (room + 1)
    tallies = tallies.at[1:1 + 2 * couples:2].set(source_of - passed).at[2:2 + 2 * couples:2].set(receiver + passed)
    return tallies[jax.random.permutation(jax.random.fold_in(key, 2), amount)]


def noise(own_key, dims, scale, limit, cuts=(), kind=jnp.bfloat16):
    values = scale * jax.random.normal(own_key, dims, jnp.float32)
    if cuts:
        values = values * block_levels(own_key, dims, cuts, -0.22, 0.18)
    return jnp.clip(values, -limit, limit).astype(kind)


def noise_with(key, dims, scale, bound, shards, heavy, kind=jnp.bfloat16):
    drawn = scale * jax.random.normal(key, dims, jnp.float32)
    if shards:
        drawn = drawn * block_levels(key, dims, shards, -0.22, 0.18)
    return jnp.clip(spiked(drawn, jax.random.fold_in(key, 3), *heavy), -bound, bound).astype(kind)


def setup_inputs(seed: int = 0) -> dict:
    seeds = jax.random.split(jax.random.key(seed), 10)
    memory = noise_with(seeds[0], (MEM_ROWS, D), 1.0, 6.0, ((0, 32),), (0, 1, 32, 2.75))
    key_weight = noise(seeds[1], (D, H * HD), D ** -0.5, 0.09375, ((0, 32), (1, 4)))
    value_weight = noise(seeds[2], (D, H * HD), D ** -0.5, 0.09375, ((0, 32), (1, 4)))
    query = draw_query(jax.random.fold_in(seeds[9], 71), 0)
    grad_context = draw_grad_context(jax.random.fold_in(seeds[9], 71), 0)
    target_segment = jax.vmap(lambda own: jnp.searchsorted(jnp.cumsum(ragged(own, EXT, TGT, QP, 1)), jnp.arange(TGT), side="right"))(jax.random.split(seeds[5], N_DP)).reshape((N_DP, TGT)).astype(jnp.int32)
    memory_segment = jax.vmap(lambda own: jnp.searchsorted(jnp.cumsum(ragged(own, EXT, M_DEV, MAXM, 1)), jnp.arange(M_DEV), side="right"))(jax.random.split(seeds[6], N_DP)).reshape((N_DP, M_DEV)).astype(jnp.int32)
    example_pack = draw_example_pack(jax.random.fold_in(seeds[9], 71), 0)
    example_slot = draw_example_slot(jax.random.fold_in(seeds[9], 71), 0)
    return dict(memory=memory, key_weight=key_weight, value_weight=value_weight, query=query, grad_context=grad_context, target_segment=target_segment, memory_segment=memory_segment, example_pack=example_pack, example_slot=example_slot)


SCORE_SCALE = 0.0625
MASKED_SCORE = -1e30


def reference(memory, key_weight, value_weight, query, grad_context, target_segment, memory_segment, example_pack, example_slot):
    width = H * HD
    joined = jnp.concatenate([key_weight, value_weight], axis=1)
    projected = jnp.dot(memory, joined, preferred_element_type=jnp.float32)
    key_packs = projected[:, :width].astype(jnp.bfloat16).reshape(N_DP, M_DEV, H, HD)
    value_packs = projected[:, width:].astype(jnp.bfloat16).reshape(N_DP, M_DEV, H, HD)
    query_packs = query.reshape(N_DP, TGT, H, HD)
    grad_packs = grad_context.reshape(N_DP, TGT, H, HD)
    example_ids = jnp.arange(EXT, dtype=jnp.int32)

    def one_target(carry, inputs):
        queries, grads, segment, packs, slots = inputs
        member = (segment[None, :] == example_ids[:, None]).astype(jnp.int32)
        counts = jnp.sum(member, axis=1).astype(jnp.int32)
        starts = (jnp.cumsum(counts) - counts).astype(jnp.int32)

        def one_example(inner, example):
            acc_keys, acc_values, context, grad_query = inner
            pack_index = lax.dynamic_index_in_dim(packs, example, 0, keepdims=False).astype(jnp.int32)
            slot_value = lax.dynamic_index_in_dim(slots, example, 0, keepdims=False)
            start = jnp.clip(lax.dynamic_index_in_dim(starts, example, 0, keepdims=False), 0, TGT - QP).astype(jnp.int32)
            query_full = lax.dynamic_slice_in_dim(queries, start, QP, 0).astype(jnp.float32)
            grad_full = lax.dynamic_slice_in_dim(grads, start, QP, 0).astype(jnp.float32)
            seg_window = lax.dynamic_slice_in_dim(segment, start, QP, 0)
            key_full = lax.dynamic_index_in_dim(key_packs, pack_index, 0, keepdims=False).astype(jnp.float32)
            value_full = lax.dynamic_index_in_dim(value_packs, pack_index, 0, keepdims=False).astype(jnp.float32)
            mem_segment = lax.dynamic_index_in_dim(memory_segment, pack_index, 0, keepdims=False)
            valid = (seg_window == example)[:, None] & (mem_segment == slot_value)[None, :]
            scores = jnp.einsum('rhd,khd->hrk', query_full, key_full) * SCORE_SCALE
            scores = jnp.where(valid[None], scores, MASKED_SCORE)
            row_top = jnp.max(scores, axis=-1, keepdims=True)
            raised = jnp.where(valid[None], jnp.exp(scores - row_top), 0.0)
            row_total = jnp.sum(raised, axis=-1, keepdims=True)
            probability = raised / jnp.where(row_total > 0.0, row_total, 1.0)
            rounded = lax.optimization_barrier(probability.astype(jnp.bfloat16)).astype(jnp.float32)
            ctx_piece = jnp.einsum('hrk,khd->rhd', rounded, value_full)
            grad_prob = jnp.einsum('rhd,khd->hrk', grad_full, value_full)
            row_delta = jnp.sum(probability * grad_prob, axis=-1, keepdims=True)
            grad_scores = probability * (grad_prob - row_delta) * SCORE_SCALE
            grad_scores = lax.optimization_barrier(grad_scores.astype(jnp.bfloat16)).astype(jnp.float32)
            gq_piece = jnp.einsum('hrk,khd->rhd', grad_scores, key_full)
            old_ctx = lax.dynamic_slice_in_dim(context, start, QP, 0)
            context = lax.dynamic_update_slice_in_dim(context, old_ctx + ctx_piece, start, 0)
            old_gq = lax.dynamic_slice_in_dim(grad_query, start, QP, 0)
            grad_query = lax.dynamic_update_slice_in_dim(grad_query, old_gq + gq_piece, start, 0)
            key_add = jnp.einsum('hrk,rhd->khd', grad_scores, query_full)
            value_add = jnp.einsum('hrk,rhd->khd', rounded, grad_full)
            old_keys = lax.dynamic_slice_in_dim(acc_keys, pack_index, 1, 0)
            acc_keys = lax.dynamic_update_slice_in_dim(acc_keys, old_keys + key_add[None], pack_index, 0)
            old_values = lax.dynamic_slice_in_dim(acc_values, pack_index, 1, 0)
            acc_values = lax.dynamic_update_slice_in_dim(acc_values, old_values + value_add[None], pack_index, 0)
            return (acc_keys, acc_values, context, grad_query), None

        acc_keys, acc_values = carry
        start_ctx = jnp.zeros((TGT, H, HD), jnp.float32)
        start_gq = jnp.zeros((TGT, H, HD), jnp.float32)
        (acc_keys, acc_values, context, grad_query), _ = lax.scan(
            one_example, (acc_keys, acc_values, start_ctx, start_gq), example_ids)
        return (acc_keys, acc_values), (context.astype(jnp.bfloat16), grad_query.astype(jnp.bfloat16))

    start_keys = jnp.zeros((N_DP, M_DEV, H, HD), jnp.float32)
    start_values = jnp.zeros((N_DP, M_DEV, H, HD), jnp.float32)
    (acc_keys, acc_values), (contexts, grad_queries) = lax.scan(
        one_target, (start_keys, start_values),
        (query_packs, grad_packs, target_segment, example_pack, example_slot))
    grad_kv = jnp.concatenate([
        acc_keys.astype(jnp.bfloat16).reshape(N_DP * M_DEV, width),
        acc_values.astype(jnp.bfloat16).reshape(N_DP * M_DEV, width)], axis=1)
    grad_memory = jnp.dot(grad_kv, joined.T, preferred_element_type=jnp.float32).astype(jnp.bfloat16)
    memory_packs = memory.reshape(N_DP, M_DEV, D)
    grad_kv_packs = grad_kv.reshape(N_DP, M_DEV, 2 * width)

    def add_pack(running, pair):
        mem_rows, grad_rows = pair
        term = jnp.dot(mem_rows.T, grad_rows, preferred_element_type=jnp.float32)
        return running + lax.optimization_barrier(term.astype(jnp.bfloat16)).astype(jnp.float32), None

    weight_grads, _ = lax.scan(add_pack, jnp.zeros((D, 2 * width), jnp.float32), (memory_packs, grad_kv_packs))
    return (contexts.reshape(N_DP * TGT, width), grad_queries.reshape(N_DP * TGT, width),
            weight_grads[:, :width], weight_grads[:, width:], grad_memory)
```

```python
import jax
import jax.numpy as jnp
from jax import lax
from jax.experimental import pallas as pl
from jax.experimental.pallas import tpu as pltpu
from jax.sharding import PartitionSpec as P

HD = 256
PEERS = 32
DEPTH = 32
BLOCK_PEERS = 8


SCORE_SCALE = 0.0625
MASKED_SCORE = -1e30


def dot(left, right, left_dim, right_dim):
    return lax.dot_general(
        left, right, (((left_dim,), (right_dim,)), ((), ())), preferred_element_type=jnp.float32
    )


def target_slots(segment, my_packs):
    rows = segment.shape[0]
    earlier = jnp.sum((segment[None, :] < segment[:, None]).astype(jnp.int32), axis=1)
    example_ids = jnp.arange(my_packs.shape[0], dtype=jnp.int32)
    pack = jnp.sum(
        jnp.where(segment[:, None] == example_ids[None, :], my_packs[None, :], 0), axis=1
    )
    return pack * DEPTH + jnp.arange(rows, dtype=jnp.int32) - earlier


def pack_body(slot_ref, query_ref, grad_ref, out_ref):
    block = pl.program_id(0)
    rows = BLOCK_PEERS * DEPTH
    positions = block * rows + lax.broadcasted_iota(jnp.int32, (rows, slot_ref.shape[1]), 0)
    chosen = jnp.where(positions == slot_ref[...], 1.0, 0.0).astype(jnp.bfloat16)
    for part, source in enumerate((query_ref, grad_ref)):
        taken = dot(chosen, source[...], 1, 0).astype(jnp.bfloat16)
        out_ref[:, part] = taken.reshape(BLOCK_PEERS, DEPTH, taken.shape[1])


def pack_slots(slots, query, grad_context):
    rows, width = query.shape
    return pl.pallas_call(
        pack_body,
        grid=(PEERS // BLOCK_PEERS,),
        in_specs=[
            pl.BlockSpec((1, rows), lambda i: (0, 0)),
            pl.BlockSpec((rows, width), lambda i: (0, 0)),
            pl.BlockSpec((rows, width), lambda i: (0, 0)),
        ],
        out_specs=pl.BlockSpec((BLOCK_PEERS, 2, DEPTH, width), lambda i: (i, 0, 0, 0)),
        out_shape=jax.ShapeDtypeStruct((PEERS, 2, DEPTH, width), jnp.bfloat16),
        name="pack_slots",
    )(slots.reshape(1, rows), query, grad_context)


def unpack_body(slot_ref, in_ref, context_ref, grad_ref):
    slots = PEERS * DEPTH
    positions = lax.broadcasted_iota(jnp.int32, (slot_ref.shape[0], slots), 1)
    chosen = jnp.where(positions == slot_ref[...], 1.0, 0.0).astype(jnp.bfloat16)
    for part, target in enumerate((context_ref, grad_ref)):
        data = in_ref[:, part].reshape(slots, in_ref.shape[3])
        target[...] = dot(chosen, data, 1, 0).astype(jnp.bfloat16)


def unpack_slots(slots, returned):
    rows = slots.shape[0]
    width = returned.shape[3]
    half = width // 2
    return pl.pallas_call(
        unpack_body,
        grid=(2,),
        in_specs=[
            pl.BlockSpec((rows, 1), lambda i: (0, 0)),
            pl.BlockSpec((PEERS, 2, DEPTH, half), lambda i: (0, 0, 0, i)),
        ],
        out_specs=[
            pl.BlockSpec((rows, half), lambda i: (0, i)),
            pl.BlockSpec((rows, half), lambda i: (0, i)),
        ],
        out_shape=[jax.ShapeDtypeStruct((rows, width), jnp.bfloat16)] * 2,
        name="unpack_slots",
    )(slots.reshape(rows, 1), returned)


def attend_body(
    wanted_ref, segment_ref, in_ref, key_ref, value_ref, out_ref, grad_kv_ref, key_sum, value_sum
):
    block = pl.program_id(1)
    rows = BLOCK_PEERS * DEPTH
    query = in_ref[:, 0].reshape(rows, HD)
    grad = in_ref[:, 1].reshape(rows, HD)
    keys = key_ref[...]
    values = value_ref[...]
    valid = wanted_ref[...] == segment_ref[...]
    scores = jnp.where(valid, dot(query, keys, 1, 1) * SCORE_SCALE, MASKED_SCORE)
    grad_prob = dot(grad, values, 1, 1)
    raised = jnp.exp(scores - jnp.max(scores, axis=1, keepdims=True))
    probability = raised / jnp.sum(raised, axis=1, keepdims=True)
    rounded = probability.astype(jnp.bfloat16)
    row_delta = jnp.sum(probability * grad_prob, axis=1, keepdims=True)
    grad_scores = (probability * (grad_prob - row_delta) * SCORE_SCALE).astype(jnp.bfloat16)
    context = dot(rounded, values, 1, 0).astype(jnp.bfloat16)
    out_ref[:, 0] = context.reshape(BLOCK_PEERS, DEPTH, HD)
    grad_query = dot(grad_scores, keys, 1, 0).astype(jnp.bfloat16)
    out_ref[:, 1] = grad_query.reshape(BLOCK_PEERS, DEPTH, HD)
    key_term = dot(grad_scores, query, 0, 0)
    value_term = dot(rounded, grad, 0, 0)

    @pl.when(block == 0)
    def _():
        key_sum[...] = key_term
        value_sum[...] = value_term

    @pl.when(block > 0)
    def _():
        key_sum[...] += key_term
        value_sum[...] += value_term

    @pl.when(block == pl.num_programs(1) - 1)
    def _():
        grad_kv_ref[0] = key_sum[...].astype(jnp.bfloat16)
        grad_kv_ref[1] = value_sum[...].astype(jnp.bfloat16)


def attend(wanted, segment, arrived, kv):
    memory_rows = segment.shape[0]
    width = arrived.shape[3]
    heads = width // HD
    rows = BLOCK_PEERS * DEPTH
    wanted_rows = jnp.broadcast_to(wanted[:, None], (PEERS, DEPTH)).reshape(PEERS * DEPTH, 1)
    return pl.pallas_call(
        attend_body,
        grid=(heads, PEERS // BLOCK_PEERS),
        in_specs=[
            pl.BlockSpec((rows, 1), lambda h, i: (i, 0)),
            pl.BlockSpec((1, memory_rows), lambda h, i: (0, 0)),
            pl.BlockSpec((BLOCK_PEERS, 2, DEPTH, HD), lambda h, i: (i, 0, 0, h)),
            pl.BlockSpec((memory_rows, HD), lambda h, i: (0, h)),
            pl.BlockSpec((memory_rows, HD), lambda h, i: (0, heads + h)),
        ],
        out_specs=[
            pl.BlockSpec((BLOCK_PEERS, 2, DEPTH, HD), lambda h, i: (i, 0, 0, h)),
            pl.BlockSpec((2, memory_rows, HD), lambda h, i: (0, 0, h)),
        ],
        out_shape=[
            jax.ShapeDtypeStruct(arrived.shape, jnp.bfloat16),
            jax.ShapeDtypeStruct((2, memory_rows, width), jnp.bfloat16),
        ],
        scratch_shapes=[pltpu.VMEM((memory_rows, HD), jnp.float32)] * 2,
        name="attend",
    )(wanted_rows, segment.reshape(1, memory_rows), arrived, kv, kv)


def per_device(
    memory,
    key_weight,
    value_weight,
    query,
    grad_context,
    target_segment,
    memory_segment,
    example_pack,
    example_slot,
):
    my_index = lax.axis_index("dp")
    width = key_weight.shape[1]
    stacked = jnp.concatenate((key_weight, value_weight), axis=1)
    weights = lax.all_gather(stacked, "dp", axis=0, tiled=True)
    my_packs = lax.dynamic_index_in_dim(example_pack, my_index, 0, keepdims=False)
    slots = target_slots(target_segment[0], my_packs)
    outgoing = pack_slots(slots, query, grad_context)
    arrived = lax.all_to_all(outgoing, "dp", split_axis=0, concat_axis=0, tiled=True)
    owned = example_pack == my_index
    wanted = jnp.where(
        jnp.any(owned, axis=1), jnp.sum(jnp.where(owned, example_slot, 0), axis=1), -1
    )
    kv = dot(memory, weights, 1, 0).astype(jnp.bfloat16)
    answers, grad_kv = attend(wanted, memory_segment[0], arrived, kv)
    grad_kv = jnp.concatenate((grad_kv[0], grad_kv[1]), axis=1)
    weight_terms = dot(memory, grad_kv, 0, 0).astype(jnp.bfloat16)
    weight_grads = lax.psum_scatter(
        weight_terms, "dp", scatter_dimension=0, tiled=True
    ).astype(jnp.float32)
    returned = lax.all_to_all(answers, "dp", split_axis=0, concat_axis=0, tiled=True)
    context, grad_query = unpack_slots(slots, returned)
    partial_sums = dot(grad_kv, weights, 1, 1).astype(jnp.bfloat16)
    grad_memory = lax.psum_scatter(partial_sums, "fsdp", scatter_dimension=0, tiled=True)
    return (
        context,
        grad_query,
        weight_grads[:, :width],
        weight_grads[:, width:],
        grad_memory,
    )


def solution(mesh):
    placed = (
        P("dp", None),
        P("dp", "fsdp"),
        P("dp", "fsdp"),
        P("dp", "fsdp"),
        P("dp", "fsdp"),
        P("dp", None),
        P("dp", None),
        P(),
        P(),
    )
    return jax.shard_map(
        per_device,
        mesh=mesh,
        in_specs=placed,
        out_specs=(
            P("dp", "fsdp"),
            P("dp", "fsdp"),
            P("dp", "fsdp"),
            P("dp", "fsdp"),
            P(("dp", "fsdp"), None),
        ),
        check_vma=False,
    )
```

```python
import jax
import jax.numpy as jnp
from jax import lax
from jax.experimental import pallas as pl
from jax.experimental.pallas import tpu as pltpu
from jax.sharding import PartitionSpec as P

HD = 256
PEERS = 32
DEPTH = 32
BLOCK_PEERS = 8


SCORE_SCALE = 0.0625
MASKED_SCORE = -1e30


def dot(left, right, left_dim, right_dim):
    return lax.dot_general(
        left, right, (((left_dim,), (right_dim,)), ((), ())), preferred_element_type=jnp.float32
    )


def target_slots(segment, my_packs):
    rows = segment.shape[0]
    earlier = jnp.sum((segment[None, :] < segment[:, None]).astype(jnp.int32), axis=1)
    example_ids = jnp.arange(my_packs.shape[0], dtype=jnp.int32)
    pack = jnp.sum(
        jnp.where(segment[:, None] == example_ids[None, :], my_packs[None, :], 0), axis=1
    )
    return pack * DEPTH + jnp.arange(rows, dtype=jnp.int32) - earlier


def pack_body(slot_ref, query_ref, grad_ref, out_ref):
    block = pl.program_id(0)
    rows = BLOCK_PEERS * DEPTH
    positions = block * rows + lax.broadcasted_iota(jnp.int32, (rows, slot_ref.shape[1]), 0)
    chosen = jnp.where(positions == slot_ref[...], 1.0, 0.0).astype(jnp.bfloat16)
    for part, source in enumerate((query_ref, grad_ref)):
        taken = dot(chosen, source[...], 1, 0).astype(jnp.bfloat16)
        out_ref[:, part] = taken.reshape(BLOCK_PEERS, DEPTH, taken.shape[1])


def pack_slots(slots, query, grad_context):
    rows, width = query.shape
    return pl.pallas_call(
        pack_body,
        grid=(PEERS // BLOCK_PEERS,),
        in_specs=[
            pl.BlockSpec((1, rows), lambda i: (0, 0)),
            pl.BlockSpec((rows, width), lambda i: (0, 0)),
            pl.BlockSpec((rows, width), lambda i: (0, 0)),
        ],
        out_specs=pl.BlockSpec((BLOCK_PEERS, 2, DEPTH, width), lambda i: (i, 0, 0, 0)),
        out_shape=jax.ShapeDtypeStruct((PEERS, 2, DEPTH, width), jnp.bfloat16),
        name="pack_slots",
    )(slots.reshape(1, rows), query, grad_context)


def unpack_body(slot_ref, in_ref, context_ref, grad_ref):
    slots = PEERS * DEPTH
    positions = lax.broadcasted_iota(jnp.int32, (slot_ref.shape[0], slots), 1)
    chosen = jnp.where(positions == slot_ref[...], 1.0, 0.0).astype(jnp.bfloat16)
    for part, target in enumerate((context_ref, grad_ref)):
        data = in_ref[:, part].reshape(slots, in_ref.shape[3])
        target[...] = dot(chosen, data, 1, 0).astype(jnp.bfloat16)


def unpack_slots(slots, returned):
    rows = slots.shape[0]
    width = returned.shape[3]
    half = width // 2
    return pl.pallas_call(
        unpack_body,
        grid=(2,),
        in_specs=[
            pl.BlockSpec((rows, 1), lambda i: (0, 0)),
            pl.BlockSpec((PEERS, 2, DEPTH, half), lambda i: (0, 0, 0, i)),
        ],
        out_specs=[
            pl.BlockSpec((rows, half), lambda i: (0, i)),
            pl.BlockSpec((rows, half), lambda i: (0, i)),
        ],
        out_shape=[jax.ShapeDtypeStruct((rows, width), jnp.bfloat16)] * 2,
        name="unpack_slots",
    )(slots.reshape(rows, 1), returned)


def attend_body(
    wanted_ref,
    segment_ref,
    in_ref,
    key_ref,
    value_ref,
    out_ref,
    grad_key_ref,
    grad_value_ref,
    key_sum,
    value_sum,
):
    block = pl.program_id(1)
    rows = BLOCK_PEERS * DEPTH
    query = in_ref[:, 0].reshape(rows, HD)
    grad = in_ref[:, 1].reshape(rows, HD)
    keys = key_ref[...]
    values = value_ref[...]
    valid = wanted_ref[...] == segment_ref[...]
    scores = jnp.where(valid, dot(query, keys, 1, 1) * SCORE_SCALE, MASKED_SCORE)
    grad_prob = dot(grad, values, 1, 1)
    raised = jnp.exp(scores - jnp.max(scores, axis=1, keepdims=True))
    probability = raised / jnp.sum(raised, axis=1, keepdims=True)
    rounded = probability.astype(jnp.bfloat16)
    row_delta = jnp.sum(probability * grad_prob, axis=1, keepdims=True)
    grad_scores = (probability * (grad_prob - row_delta) * SCORE_SCALE).astype(jnp.bfloat16)
    context = dot(rounded, values, 1, 0).astype(jnp.bfloat16)
    out_ref[:, 0] = context.reshape(BLOCK_PEERS, DEPTH, HD)
    grad_query = dot(grad_scores, keys, 1, 0).astype(jnp.bfloat16)
    out_ref[:, 1] = grad_query.reshape(BLOCK_PEERS, DEPTH, HD)
    key_term = dot(grad_scores, query, 0, 0)
    value_term = dot(rounded, grad, 0, 0)

    @pl.when(block == 0)
    def _():
        key_sum[...] = key_term
        value_sum[...] = value_term

    @pl.when(block > 0)
    def _():
        key_sum[...] += key_term
        value_sum[...] += value_term

    @pl.when(block == pl.num_programs(1) - 1)
    def _():
        grad_key_ref[...] = key_sum[...].astype(jnp.bfloat16)
        grad_value_ref[...] = value_sum[...].astype(jnp.bfloat16)


def attend(wanted, segment, arrived, kv):
    memory_rows = segment.shape[0]
    width = arrived.shape[3]
    heads = width // HD
    rows = BLOCK_PEERS * DEPTH
    wanted_rows = jnp.broadcast_to(wanted[:, None], (PEERS, DEPTH)).reshape(PEERS * DEPTH, 1)
    return pl.pallas_call(
        attend_body,
        grid=(heads, PEERS // BLOCK_PEERS),
        in_specs=[
            pl.BlockSpec((rows, 1), lambda h, i: (i, 0)),
            pl.BlockSpec((1, memory_rows), lambda h, i: (0, 0)),
            pl.BlockSpec((BLOCK_PEERS, 2, DEPTH, HD), lambda h, i: (i, 0, 0, h)),
            pl.BlockSpec((memory_rows, HD), lambda h, i: (0, h)),
            pl.BlockSpec((memory_rows, HD), lambda h, i: (0, heads + h)),
        ],
        out_specs=[
            pl.BlockSpec((BLOCK_PEERS, 2, DEPTH, HD), lambda h, i: (i, 0, 0, h)),
            pl.BlockSpec((memory_rows, HD), lambda h, i: (0, h)),
            pl.BlockSpec((memory_rows, HD), lambda h, i: (0, h)),
        ],
        out_shape=[
            jax.ShapeDtypeStruct(arrived.shape, jnp.bfloat16),
            jax.ShapeDtypeStruct((memory_rows, width), jnp.bfloat16),
            jax.ShapeDtypeStruct((memory_rows, width), jnp.bfloat16),
        ],
        scratch_shapes=[pltpu.VMEM((memory_rows, HD), jnp.float32)] * 2,
        name="attend",
    )(wanted_rows, segment.reshape(1, memory_rows), arrived, kv, kv)


def weight_body(memory_ref, grad_key_ref, grad_value_ref, out_ref):
    width = grad_key_ref.shape[1]
    columns = memory_ref[...]
    out_ref[:, :width] = dot(columns, grad_key_ref[...], 0, 0).astype(jnp.bfloat16)
    out_ref[:, width:] = dot(columns, grad_value_ref[...], 0, 0).astype(jnp.bfloat16)


def weight_terms(memory, grad_keys, grad_values):
    rows, model = memory.shape
    width = grad_keys.shape[1]
    block = 512
    return pl.pallas_call(
        weight_body,
        grid=(model // block,),
        in_specs=[
            pl.BlockSpec((rows, block), lambda i: (0, i)),
            pl.BlockSpec((rows, width), lambda i: (0, 0)),
            pl.BlockSpec((rows, width), lambda i: (0, 0)),
        ],
        out_specs=pl.BlockSpec((block, 2 * width), lambda i: (i, 0)),
        out_shape=jax.ShapeDtypeStruct((model, 2 * width), jnp.bfloat16),
        name="weight_terms",
    )(memory, grad_keys, grad_values)


def memory_body(grad_key_ref, grad_value_ref, weight_ref, out_ref):
    width = grad_key_ref.shape[1]
    total = dot(grad_key_ref[...], weight_ref[:, :width], 1, 1)
    total += dot(grad_value_ref[...], weight_ref[:, width:], 1, 1)
    out_ref[...] = total.astype(jnp.bfloat16)


def memory_terms(grad_keys, grad_values, weights):
    rows, width = grad_keys.shape
    model = weights.shape[0]
    block = 512
    return pl.pallas_call(
        memory_body,
        grid=(model // block,),
        in_specs=[
            pl.BlockSpec((rows, width), lambda i: (0, 0)),
            pl.BlockSpec((rows, width), lambda i: (0, 0)),
            pl.BlockSpec((block, 2 * width), lambda i: (i, 0)),
        ],
        out_specs=pl.BlockSpec((rows, block), lambda i: (0, i)),
        out_shape=jax.ShapeDtypeStruct((rows, model), jnp.bfloat16),
        name="memory_terms",
    )(grad_keys, grad_values, weights)


def per_device(
    memory,
    key_weight,
    value_weight,
    query,
    grad_context,
    target_segment,
    memory_segment,
    example_pack,
    example_slot,
):
    my_index = lax.axis_index("dp")
    width = key_weight.shape[1]
    stacked = jnp.concatenate((key_weight, value_weight), axis=1)
    weights = lax.all_gather(stacked, "dp", axis=0, tiled=True)
    my_packs = lax.dynamic_index_in_dim(example_pack, my_index, 0, keepdims=False)
    slots = target_slots(target_segment[0], my_packs)
    outgoing = pack_slots(slots, query, grad_context)
    arrived = lax.all_to_all(outgoing, "dp", split_axis=0, concat_axis=0, tiled=True)
    owned = example_pack == my_index
    wanted = jnp.where(
        jnp.any(owned, axis=1), jnp.sum(jnp.where(owned, example_slot, 0), axis=1), -1
    )
    kv = dot(memory, weights, 1, 0).astype(jnp.bfloat16)
    answers, grad_keys, grad_values = attend(wanted, memory_segment[0], arrived, kv)
    weight_grads = lax.psum_scatter(
        weight_terms(memory, grad_keys, grad_values), "dp", scatter_dimension=0, tiled=True
    ).astype(jnp.float32)
    returned = lax.all_to_all(answers, "dp", split_axis=0, concat_axis=0, tiled=True)
    context, grad_query = unpack_slots(slots, returned)
    terms = lax.all_to_all(
        memory_terms(grad_keys, grad_values, weights),
        "fsdp",
        split_axis=0,
        concat_axis=0,
        tiled=True,
    )
    groups = lax.axis_size("fsdp")
    grad_memory = jnp.sum(
        terms.reshape(groups, terms.shape[0] // groups, terms.shape[1]).astype(jnp.float32), axis=0
    ).astype(jnp.bfloat16)
    return (
        context,
        grad_query,
        weight_grads[:, :width],
        weight_grads[:, width:],
        grad_memory,
    )


def solution(mesh):
    placed = (
        P("dp", None),
        P("dp", "fsdp"),
        P("dp", "fsdp"),
        P("dp", "fsdp"),
        P("dp", "fsdp"),
        P("dp", None),
        P("dp", None),
        P(),
        P(),
    )
    return jax.shard_map(
        per_device,
        mesh=mesh,
        in_specs=placed,
        out_specs=(
            P("dp", "fsdp"),
            P("dp", "fsdp"),
            P("dp", "fsdp"),
            P("dp", "fsdp"),
            P(("dp", "fsdp"), None),
        ),
        check_vma=False,
    )
```

```python
import jax
import jax.numpy as jnp
from jax import lax
from jax.experimental import pallas as pl
from jax.experimental.pallas import tpu as pltpu
from jax.sharding import PartitionSpec as P

HD = 256
PEERS = 32
DEPTH = 32
BLOCK_PEERS = 8
RING = 4


SCORE_SCALE = 0.0625
MASKED_SCORE = -1e30


def dot(left, right, left_dim, right_dim):
    return lax.dot_general(
        left, right, (((left_dim,), (right_dim,)), ((), ())), preferred_element_type=jnp.float32
    )


def target_slots(segment, my_packs):
    rows = segment.shape[0]
    earlier = jnp.sum((segment[None, :] < segment[:, None]).astype(jnp.int32), axis=1)
    example_ids = jnp.arange(my_packs.shape[0], dtype=jnp.int32)
    pack = jnp.sum(
        jnp.where(segment[:, None] == example_ids[None, :], my_packs[None, :], 0), axis=1
    )
    return pack * DEPTH + jnp.arange(rows, dtype=jnp.int32) - earlier


def pack_body(slot_ref, query_ref, grad_ref, out_ref):
    block = pl.program_id(0)
    rows = BLOCK_PEERS * DEPTH
    positions = block * rows + lax.broadcasted_iota(jnp.int32, (rows, slot_ref.shape[1]), 0)
    chosen = jnp.where(positions == slot_ref[...], 1.0, 0.0).astype(jnp.bfloat16)
    for part, source in enumerate((query_ref, grad_ref)):
        taken = dot(chosen, source[...], 1, 0).astype(jnp.bfloat16)
        out_ref[:, part] = taken.reshape(BLOCK_PEERS, DEPTH, taken.shape[1])


def pack_slots(slots, query, grad_context):
    rows, width = query.shape
    return pl.pallas_call(
        pack_body,
        grid=(PEERS // BLOCK_PEERS,),
        in_specs=[
            pl.BlockSpec((1, rows), lambda i: (0, 0)),
            pl.BlockSpec((rows, width), lambda i: (0, 0)),
            pl.BlockSpec((rows, width), lambda i: (0, 0)),
        ],
        out_specs=pl.BlockSpec((BLOCK_PEERS, 2, DEPTH, width), lambda i: (i, 0, 0, 0)),
        out_shape=jax.ShapeDtypeStruct((PEERS, 2, DEPTH, width), jnp.bfloat16),
        name="pack_slots",
    )(slots.reshape(1, rows), query, grad_context)


def unpack_body(slot_ref, in_ref, context_ref, grad_ref):
    slots = PEERS * DEPTH
    positions = lax.broadcasted_iota(jnp.int32, (slot_ref.shape[0], slots), 1)
    chosen = jnp.where(positions == slot_ref[...], 1.0, 0.0).astype(jnp.bfloat16)
    for part, target in enumerate((context_ref, grad_ref)):
        data = in_ref[:, part].reshape(slots, in_ref.shape[3])
        target[...] = dot(chosen, data, 1, 0).astype(jnp.bfloat16)


def unpack_slots(slots, returned):
    rows = slots.shape[0]
    width = returned.shape[3]
    half = width // 2
    return pl.pallas_call(
        unpack_body,
        grid=(2,),
        in_specs=[
            pl.BlockSpec((rows, 1), lambda i: (0, 0)),
            pl.BlockSpec((PEERS, 2, DEPTH, half), lambda i: (0, 0, 0, i)),
        ],
        out_specs=[
            pl.BlockSpec((rows, half), lambda i: (0, i)),
            pl.BlockSpec((rows, half), lambda i: (0, i)),
        ],
        out_shape=[jax.ShapeDtypeStruct((rows, width), jnp.bfloat16)] * 2,
        name="unpack_slots",
    )(slots.reshape(rows, 1), returned)


def attend_body(
    wanted_ref,
    segment_ref,
    in_ref,
    key_ref,
    value_ref,
    out_ref,
    grad_key_ref,
    grad_value_ref,
    key_sum,
    value_sum,
):
    block = pl.program_id(1)
    rows = BLOCK_PEERS * DEPTH
    query = in_ref[:, 0].reshape(rows, HD)
    grad = in_ref[:, 1].reshape(rows, HD)
    keys = key_ref[...]
    values = value_ref[...]
    valid = wanted_ref[...] == segment_ref[...]
    scores = jnp.where(valid, dot(query, keys, 1, 1) * SCORE_SCALE, MASKED_SCORE)
    grad_prob = dot(grad, values, 1, 1)
    raised = jnp.exp(scores - jnp.max(scores, axis=1, keepdims=True))
    probability = raised / jnp.sum(raised, axis=1, keepdims=True)
    rounded = probability.astype(jnp.bfloat16)
    row_delta = jnp.sum(probability * grad_prob, axis=1, keepdims=True)
    grad_scores = (probability * (grad_prob - row_delta) * SCORE_SCALE).astype(jnp.bfloat16)
    context = dot(rounded, values, 1, 0).astype(jnp.bfloat16)
    out_ref[:, 0] = context.reshape(BLOCK_PEERS, DEPTH, HD)
    grad_query = dot(grad_scores, keys, 1, 0).astype(jnp.bfloat16)
    out_ref[:, 1] = grad_query.reshape(BLOCK_PEERS, DEPTH, HD)
    key_term = dot(grad_scores, query, 0, 0)
    value_term = dot(rounded, grad, 0, 0)

    @pl.when(block == 0)
    def _():
        key_sum[...] = key_term
        value_sum[...] = value_term

    @pl.when(block > 0)
    def _():
        key_sum[...] += key_term
        value_sum[...] += value_term

    @pl.when(block == pl.num_programs(1) - 1)
    def _():
        grad_key_ref[...] = key_sum[...].astype(jnp.bfloat16)
        grad_value_ref[...] = value_sum[...].astype(jnp.bfloat16)


def attend(wanted, segment, arrived, kv):
    memory_rows = segment.shape[0]
    width = arrived.shape[3]
    heads = width // HD
    rows = BLOCK_PEERS * DEPTH
    wanted_rows = jnp.broadcast_to(wanted[:, None], (PEERS, DEPTH)).reshape(PEERS * DEPTH, 1)
    return pl.pallas_call(
        attend_body,
        grid=(heads, PEERS // BLOCK_PEERS),
        in_specs=[
            pl.BlockSpec((rows, 1), lambda h, i: (i, 0)),
            pl.BlockSpec((1, memory_rows), lambda h, i: (0, 0)),
            pl.BlockSpec((BLOCK_PEERS, 2, DEPTH, HD), lambda h, i: (i, 0, 0, h)),
            pl.BlockSpec((memory_rows, HD), lambda h, i: (0, h)),
            pl.BlockSpec((memory_rows, HD), lambda h, i: (0, heads + h)),
        ],
        out_specs=[
            pl.BlockSpec((BLOCK_PEERS, 2, DEPTH, HD), lambda h, i: (i, 0, 0, h)),
            pl.BlockSpec((memory_rows, HD), lambda h, i: (0, h)),
            pl.BlockSpec((memory_rows, HD), lambda h, i: (0, h)),
        ],
        out_shape=[
            jax.ShapeDtypeStruct(arrived.shape, jnp.bfloat16),
            jax.ShapeDtypeStruct((memory_rows, width), jnp.bfloat16),
            jax.ShapeDtypeStruct((memory_rows, width), jnp.bfloat16),
        ],
        scratch_shapes=[pltpu.VMEM((memory_rows, HD), jnp.float32)] * 2,
        name="attend",
    )(wanted_rows, segment.reshape(1, memory_rows), arrived, kv, kv)


def peer_of(y, x, core):
    return (y % RING) * 2 * RING + (x % RING) * 2 + core


def shift(y_step, x_step, swap):
    return [
        (peer_of(y, x, core), peer_of(y + y_step, x + x_step, core ^ swap))
        for y in range(RING)
        for x in range(RING)
        for core in range(2)
    ]


def relative_table(core):
    index = lax.axis_index("dp")
    steps = jnp.arange(RING * RING, dtype=jnp.int32)
    return peer_of(index // (2 * RING) + steps // RING, index // 2 % RING + steps % RING, core)


def away_body(table_ref, memory_ref, grad_key_ref, grad_value_ref, out_ref):
    del table_ref
    width = grad_key_ref.shape[1]
    columns = memory_ref[...]
    out_ref[:, :width] = dot(columns, grad_key_ref[...], 0, 0).astype(jnp.bfloat16)
    out_ref[:, width:] = dot(columns, grad_value_ref[...], 0, 0).astype(jnp.bfloat16)


def away_terms(table, memory, grad_keys, grad_values):
    rows, model = memory.shape
    width = grad_keys.shape[1]
    block = model // PEERS
    steps = RING * RING
    return pl.pallas_call(
        away_body,
        grid_spec=pltpu.PrefetchScalarGridSpec(
            num_scalar_prefetch=1,
            grid=(steps,),
            in_specs=[
                pl.BlockSpec((rows, block), lambda i, table: (0, table[i])),
                pl.BlockSpec((rows, width), lambda i, table: (0, 0)),
                pl.BlockSpec((rows, width), lambda i, table: (0, 0)),
            ],
            out_specs=pl.BlockSpec((block, 2 * width), lambda i, table: (i, 0)),
        ),
        out_shape=jax.ShapeDtypeStruct((steps * block, 2 * width), jnp.bfloat16),
        name="away_terms",
    )(table, memory, grad_keys, grad_values)


def home_body(table_ref, memory_ref, grad_key_ref, grad_value_ref, other_ref, *out_refs):
    del table_ref
    y_step = pl.program_id(0)
    x_step = pl.program_id(1)
    width = grad_key_ref.shape[1]
    half = other_ref.shape[0] // 2
    columns = memory_ref[...]
    for start, grad_ref in ((0, grad_key_ref), (width, grad_value_ref)):
        total = dot(columns, grad_ref[...], 0, 0)
        total += other_ref[:, start : start + width].astype(jnp.float32)
        total = total.astype(jnp.bfloat16)
        for step in range(RING):

            @pl.when(y_step == step)
            def _():
                out_refs[step][x_step, :, start : start + width] = total[:half]

            @pl.when(x_step == step)
            def _():
                out_refs[RING + step][y_step, :, start : start + width] = total[half:]


def home_terms(table, memory, grad_keys, grad_values, other):
    rows, model = memory.shape
    width = grad_keys.shape[1]
    block = model // PEERS
    piece = (RING, block // 2, 2 * width)
    return pl.pallas_call(
        home_body,
        grid_spec=pltpu.PrefetchScalarGridSpec(
            num_scalar_prefetch=1,
            grid=(RING, RING),
            in_specs=[
                pl.BlockSpec((rows, block), lambda i, j, table: (0, table[i * RING + j])),
                pl.BlockSpec((rows, width), lambda i, j, table: (0, 0)),
                pl.BlockSpec((rows, width), lambda i, j, table: (0, 0)),
                pl.BlockSpec((block, 2 * width), lambda i, j, table: (i * RING + j, 0)),
            ],
            out_specs=[pl.BlockSpec(piece, lambda i, j, table: (0, 0, 0))] * (2 * RING),
        ),
        out_shape=[jax.ShapeDtypeStruct(piece, jnp.bfloat16)] * (2 * RING),
        name="home_terms",
    )(table, memory, grad_keys, grad_values, other)


def sum_pieces(pieces):
    total = pieces[0].astype(jnp.float32)
    for piece in pieces[1:]:
        total += piece.astype(jnp.float32)
    return total


def ring_exchange(pieces, along_y):
    received = [pieces[0]]
    for step in range(1, RING):
        perm = shift(step, 0, 0) if along_y else shift(0, step, 0)
        received.append(lax.ppermute(pieces[step], "dp", perm))
    return received


def first_sums(received):
    return [
        sum_pieces([piece[step] for piece in received]).astype(jnp.bfloat16)
        for step in range(RING)
    ]


def memory_body(group_ref, grad_key_ref, grad_value_ref, weight_ref, *refs):
    out_refs, total_ref = refs[:-1], refs[-1]
    width = grad_key_ref.shape[1]
    rows = out_refs[0].shape[0]
    total = dot(grad_key_ref[...], weight_ref[:, :width], 1, 1)
    total += dot(grad_value_ref[...], weight_ref[:, width:], 1, 1)
    total_ref[...] = total
    for step, out_ref in enumerate(out_refs):
        start = pl.multiple_of((group_ref[0] + step) % RING * rows, rows)
        out_ref[...] = total_ref[pl.ds(start, rows), :].astype(jnp.bfloat16)


def memory_terms(group, grad_keys, grad_values, weights):
    rows, width = grad_keys.shape
    model = weights.shape[0]
    block = 512
    return pl.pallas_call(
        memory_body,
        grid_spec=pltpu.PrefetchScalarGridSpec(
            num_scalar_prefetch=1,
            grid=(model // block,),
            in_specs=[
                pl.BlockSpec((rows, width), lambda i, group: (0, 0)),
                pl.BlockSpec((rows, width), lambda i, group: (0, 0)),
                pl.BlockSpec((block, 2 * width), lambda i, group: (i, 0)),
            ],
            out_specs=[pl.BlockSpec((rows // RING, block), lambda i, group: (0, i))] * RING,
            scratch_shapes=[pltpu.VMEM((rows, block), jnp.float32)],
        ),
        out_shape=[jax.ShapeDtypeStruct((rows // RING, model), jnp.bfloat16)] * RING,
        name="memory_terms",
    )(group, grad_keys, grad_values, weights)


def per_device(
    memory,
    key_weight,
    value_weight,
    query,
    grad_context,
    target_segment,
    memory_segment,
    example_pack,
    example_slot,
):
    my_index = lax.axis_index("dp")
    width = key_weight.shape[1]
    stacked = jnp.concatenate((key_weight, value_weight), axis=1)
    weights = lax.all_gather(stacked, "dp", axis=0, tiled=True)
    my_packs = lax.dynamic_index_in_dim(example_pack, my_index, 0, keepdims=False)
    slots = target_slots(target_segment[0], my_packs)
    outgoing = pack_slots(slots, query, grad_context)
    arrived = lax.all_to_all(outgoing, "dp", split_axis=0, concat_axis=0, tiled=True)
    owned = example_pack == my_index
    wanted = jnp.where(
        jnp.any(owned, axis=1), jnp.sum(jnp.where(owned, example_slot, 0), axis=1), -1
    )
    kv = dot(memory, weights, 1, 0).astype(jnp.bfloat16)
    answers, grad_keys, grad_values = attend(wanted, memory_segment[0], arrived, kv)
    returned = lax.all_to_all(answers, "dp", split_axis=0, concat_axis=0, tiled=True)
    core = my_index % 2
    away = away_terms(relative_table(1 - core), memory, grad_keys, grad_values)
    other = lax.ppermute(away, "dp", shift(0, 0, 1))
    group = lax.axis_index("fsdp").astype(jnp.int32).reshape(1)
    terms = memory_terms(group, grad_keys, grad_values, weights)
    other, terms = lax.optimization_barrier((other, terms))
    pieces = home_terms(relative_table(core), memory, grad_keys, grad_values, other)
    arrived_terms = [terms[0]] + [
        lax.ppermute(terms[step], "fsdp", [(i, (i + step) % RING) for i in range(RING)])
        for step in range(1, RING)
    ]
    context, grad_query = unpack_slots(slots, returned)
    sums_y = first_sums(ring_exchange(pieces[:RING], True))
    sums_x = first_sums(ring_exchange(pieces[RING:], False))
    weight_grads = jnp.concatenate(
        [
            sum_pieces(ring_exchange(sums_y, False)),
            sum_pieces(ring_exchange(sums_x, True)),
        ],
        axis=0,
    )
    grad_memory = sum_pieces(arrived_terms).astype(jnp.bfloat16)
    return (
        context,
        grad_query,
        weight_grads[:, :width],
        weight_grads[:, width:],
        grad_memory,
    )


def solution(mesh):
    placed = (
        P("dp", None),
        P("dp", "fsdp"),
        P("dp", "fsdp"),
        P("dp", "fsdp"),
        P("dp", "fsdp"),
        P("dp", None),
        P("dp", None),
        P(),
        P(),
    )
    return jax.shard_map(
        per_device,
        mesh=mesh,
        in_specs=placed,
        out_specs=(
            P("dp", "fsdp"),
            P("dp", "fsdp"),
            P("dp", "fsdp"),
            P("dp", "fsdp"),
            P(("dp", "fsdp"), None),
        ),
        check_vma=False,
    )
```

```python
import jax
import jax.numpy as jnp
from jax import lax
from jax.experimental import pallas as pl
from jax.experimental.pallas import tpu as pltpu
from jax.sharding import PartitionSpec as P

HD = 256
PEERS = 32
DEPTH = 32
BLOCK_PEERS = 8
RING = 4


SCORE_SCALE = 0.0625
MASKED_SCORE = -1e30


def dot(left, right, left_dim, right_dim):
    return lax.dot_general(
        left, right, (((left_dim,), (right_dim,)), ((), ())), preferred_element_type=jnp.float32
    )


def target_slots(segment, my_packs):
    rows = segment.shape[0]
    earlier = jnp.sum((segment[None, :] < segment[:, None]).astype(jnp.int32), axis=1)
    example_ids = jnp.arange(my_packs.shape[0], dtype=jnp.int32)
    pack = jnp.sum(
        jnp.where(segment[:, None] == example_ids[None, :], my_packs[None, :], 0), axis=1
    )
    return pack * DEPTH + jnp.arange(rows, dtype=jnp.int32) - earlier


def pack_body(slot_ref, query_ref, grad_ref, out_ref):
    block = pl.program_id(0)
    rows = BLOCK_PEERS * DEPTH
    positions = block * rows + lax.broadcasted_iota(jnp.int32, (rows, slot_ref.shape[1]), 0)
    chosen = jnp.where(positions == slot_ref[...], 1.0, 0.0).astype(jnp.bfloat16)
    for part, source in enumerate((query_ref, grad_ref)):
        taken = dot(chosen, source[...], 1, 0).astype(jnp.bfloat16)
        out_ref[:, part] = taken.reshape(BLOCK_PEERS, DEPTH, taken.shape[1])


def pack_slots(slots, query, grad_context):
    rows, width = query.shape
    return pl.pallas_call(
        pack_body,
        grid=(PEERS // BLOCK_PEERS,),
        in_specs=[
            pl.BlockSpec((1, rows), lambda i: (0, 0)),
            pl.BlockSpec((rows, width), lambda i: (0, 0)),
            pl.BlockSpec((rows, width), lambda i: (0, 0)),
        ],
        out_specs=pl.BlockSpec((BLOCK_PEERS, 2, DEPTH, width), lambda i: (i, 0, 0, 0)),
        out_shape=jax.ShapeDtypeStruct((PEERS, 2, DEPTH, width), jnp.bfloat16),
        name="pack_slots",
    )(slots.reshape(1, rows), query, grad_context)


def unpack_body(slot_ref, in_ref, context_ref, grad_ref):
    slots = PEERS * DEPTH
    positions = lax.broadcasted_iota(jnp.int32, (slot_ref.shape[0], slots), 1)
    chosen = jnp.where(positions == slot_ref[...], 1.0, 0.0).astype(jnp.bfloat16)
    for part, target in enumerate((context_ref, grad_ref)):
        data = in_ref[:, part].reshape(slots, in_ref.shape[3])
        target[...] = dot(chosen, data, 1, 0).astype(jnp.bfloat16)


def unpack_slots(slots, returned):
    rows = slots.shape[0]
    width = returned.shape[3]
    half = width // 2
    return pl.pallas_call(
        unpack_body,
        grid=(2,),
        in_specs=[
            pl.BlockSpec((rows, 1), lambda i: (0, 0)),
            pl.BlockSpec((PEERS, 2, DEPTH, half), lambda i: (0, 0, 0, i)),
        ],
        out_specs=[
            pl.BlockSpec((rows, half), lambda i: (0, i)),
            pl.BlockSpec((rows, half), lambda i: (0, i)),
        ],
        out_shape=[jax.ShapeDtypeStruct((rows, width), jnp.bfloat16)] * 2,
        name="unpack_slots",
    )(slots.reshape(rows, 1), returned)


def attend_body(
    wanted_ref,
    segment_ref,
    in_ref,
    key_ref,
    value_ref,
    out_ref,
    grad_key_ref,
    grad_value_ref,
    key_sum,
    value_sum,
):
    block = pl.program_id(1)
    rows = BLOCK_PEERS * DEPTH
    query = in_ref[:, 0].reshape(rows, HD)
    grad = in_ref[:, 1].reshape(rows, HD)
    keys = key_ref[...]
    values = value_ref[...]
    valid = wanted_ref[...] == segment_ref[...]
    scores = jnp.where(valid, dot(query, keys, 1, 1) * SCORE_SCALE, MASKED_SCORE)
    grad_prob = dot(grad, values, 1, 1)
    raised = jnp.exp(scores - jnp.max(scores, axis=1, keepdims=True))
    probability = raised / jnp.sum(raised, axis=1, keepdims=True)
    rounded = probability.astype(jnp.bfloat16)
    row_delta = jnp.sum(probability * grad_prob, axis=1, keepdims=True)
    grad_scores = (probability * (grad_prob - row_delta) * SCORE_SCALE).astype(jnp.bfloat16)
    context = dot(rounded, values, 1, 0).astype(jnp.bfloat16)
    out_ref[:, 0] = context.reshape(BLOCK_PEERS, DEPTH, HD)
    grad_query = dot(grad_scores, keys, 1, 0).astype(jnp.bfloat16)
    out_ref[:, 1] = grad_query.reshape(BLOCK_PEERS, DEPTH, HD)
    key_term = dot(grad_scores, query, 0, 0)
    value_term = dot(rounded, grad, 0, 0)

    @pl.when(block == 0)
    def _():
        key_sum[...] = key_term
        value_sum[...] = value_term

    @pl.when(block > 0)
    def _():
        key_sum[...] += key_term
        value_sum[...] += value_term

    @pl.when(block == pl.num_programs(1) - 1)
    def _():
        grad_key_ref[...] = key_sum[...].astype(jnp.bfloat16)
        grad_value_ref[...] = value_sum[...].astype(jnp.bfloat16)


def attend(wanted, segment, arrived, kv):
    memory_rows = segment.shape[0]
    width = arrived.shape[3]
    heads = width // HD
    rows = BLOCK_PEERS * DEPTH
    wanted_rows = jnp.broadcast_to(wanted[:, None], (PEERS, DEPTH)).reshape(PEERS * DEPTH, 1)
    return pl.pallas_call(
        attend_body,
        grid=(heads, PEERS // BLOCK_PEERS),
        in_specs=[
            pl.BlockSpec((rows, 1), lambda h, i: (i, 0)),
            pl.BlockSpec((1, memory_rows), lambda h, i: (0, 0)),
            pl.BlockSpec((BLOCK_PEERS, 2, DEPTH, HD), lambda h, i: (i, 0, 0, h)),
            pl.BlockSpec((memory_rows, HD), lambda h, i: (0, h)),
            pl.BlockSpec((memory_rows, HD), lambda h, i: (0, heads + h)),
        ],
        out_specs=[
            pl.BlockSpec((BLOCK_PEERS, 2, DEPTH, HD), lambda h, i: (i, 0, 0, h)),
            pl.BlockSpec((memory_rows, HD), lambda h, i: (0, h)),
            pl.BlockSpec((memory_rows, HD), lambda h, i: (0, h)),
        ],
        out_shape=[
            jax.ShapeDtypeStruct(arrived.shape, jnp.bfloat16),
            jax.ShapeDtypeStruct((memory_rows, width), jnp.bfloat16),
            jax.ShapeDtypeStruct((memory_rows, width), jnp.bfloat16),
        ],
        scratch_shapes=[pltpu.VMEM((memory_rows, HD), jnp.float32)] * 2,
        name="attend",
    )(wanted_rows, segment.reshape(1, memory_rows), arrived, kv, kv)


def peer_of(y, x, core):
    return (y % RING) * 2 * RING + (x % RING) * 2 + core


def shift(y_step, x_step, swap):
    return [
        (peer_of(y, x, core), peer_of(y + y_step, x + x_step, core ^ swap))
        for y in range(RING)
        for x in range(RING)
        for core in range(2)
    ]


def relative_table(core):
    index = lax.axis_index("dp")
    steps = jnp.arange(RING * RING, dtype=jnp.int32)
    return peer_of(index // (2 * RING) + steps // RING, index // 2 % RING + steps % RING, core)


def joined_columns(refs):
    return jnp.concatenate([ref[...] for ref in refs], axis=1)


def column_specs(rows, block):
    return [
        pl.BlockSpec((rows, block), lambda i, table, j=j: (0, table[i * RING + j]))
        for j in range(RING)
    ]


def away_body(table_ref, *refs):
    del table_ref
    grad_key_ref, grad_value_ref, out_ref = refs[RING:]
    width = grad_key_ref.shape[1]
    columns = joined_columns(refs[:RING])
    out_ref[:, :width] = dot(columns, grad_key_ref[...], 0, 0).astype(jnp.bfloat16)
    out_ref[:, width:] = dot(columns, grad_value_ref[...], 0, 0).astype(jnp.bfloat16)


def away_terms(table, memory, grad_keys, grad_values):
    rows, model = memory.shape
    width = grad_keys.shape[1]
    block = model // PEERS
    return pl.pallas_call(
        away_body,
        grid_spec=pltpu.PrefetchScalarGridSpec(
            num_scalar_prefetch=1,
            grid=(RING,),
            in_specs=column_specs(rows, block)
            + [
                pl.BlockSpec((rows, width), lambda i, table: (0, 0)),
                pl.BlockSpec((rows, width), lambda i, table: (0, 0)),
            ],
            out_specs=pl.BlockSpec((RING * block, 2 * width), lambda i, table: (i, 0)),
        ),
        out_shape=jax.ShapeDtypeStruct((model // 2, 2 * width), jnp.bfloat16),
        name="away_terms",
    )(table, *([memory] * RING), grad_keys, grad_values)


def home_body(table_ref, *refs):
    del table_ref
    grad_key_ref, grad_value_ref, other_ref = refs[RING : RING + 3]
    out_refs = refs[RING + 3 :]
    y_step = pl.program_id(0)
    width = grad_key_ref.shape[1]
    half = out_refs[0].shape[1]
    columns = joined_columns(refs[:RING])
    for start, grad_ref in ((0, grad_key_ref), (width, grad_value_ref)):
        total = dot(columns, grad_ref[...], 0, 0)
        total += other_ref[:, start : start + width].astype(jnp.float32)
        total = total.astype(jnp.bfloat16).reshape(RING, 2 * half, width)
        for step in range(RING):
            out_refs[RING + step][y_step, :, start : start + width] = total[step, half:]

            @pl.when(y_step == step)
            def _():
                out_refs[step][:, :, start : start + width] = total[:, :half]


def home_terms(table, memory, grad_keys, grad_values, other):
    rows, model = memory.shape
    width = grad_keys.shape[1]
    block = model // PEERS
    piece = (RING, block // 2, 2 * width)
    return pl.pallas_call(
        home_body,
        grid_spec=pltpu.PrefetchScalarGridSpec(
            num_scalar_prefetch=1,
            grid=(RING,),
            in_specs=column_specs(rows, block)
            + [
                pl.BlockSpec((rows, width), lambda i, table: (0, 0)),
                pl.BlockSpec((rows, width), lambda i, table: (0, 0)),
                pl.BlockSpec((RING * block, 2 * width), lambda i, table: (i, 0)),
            ],
            out_specs=[pl.BlockSpec(piece, lambda i, table: (0, 0, 0))] * (2 * RING),
        ),
        out_shape=[jax.ShapeDtypeStruct(piece, jnp.bfloat16)] * (2 * RING),
        name="home_terms",
    )(table, *([memory] * RING), grad_keys, grad_values, other)


def sum_pieces(pieces):
    total = pieces[0].astype(jnp.float32)
    for piece in pieces[1:]:
        total += piece.astype(jnp.float32)
    return total


def ring_exchange(pieces, along_y):
    received = [pieces[0]]
    for step in range(1, RING):
        perm = shift(step, 0, 0) if along_y else shift(0, step, 0)
        received.append(lax.ppermute(pieces[step], "dp", perm))
    return received


def first_sums(received):
    return [
        sum_pieces([piece[step] for piece in received]).astype(jnp.bfloat16)
        for step in range(RING)
    ]


def memory_body(grad_key_ref, grad_value_ref, weight_ref, out_ref):
    width = grad_key_ref.shape[1]
    total = dot(grad_key_ref[...], weight_ref[:, :width], 1, 1)
    total += dot(grad_value_ref[...], weight_ref[:, width:], 1, 1)
    out_ref[...] = total.astype(jnp.bfloat16)


def memory_terms(grad_keys, grad_values, weights):
    rows, width = grad_keys.shape
    model = weights.shape[0]
    block = 512
    return pl.pallas_call(
        memory_body,
        grid=(model // block,),
        in_specs=[
            pl.BlockSpec((rows, width), lambda i: (0, 0)),
            pl.BlockSpec((rows, width), lambda i: (0, 0)),
            pl.BlockSpec((block, 2 * width), lambda i: (i, 0)),
        ],
        out_specs=pl.BlockSpec((rows, block), lambda i: (0, i)),
        out_shape=jax.ShapeDtypeStruct((rows, model), jnp.bfloat16),
        name="memory_terms",
    )(grad_keys, grad_values, weights)


def per_device(
    memory,
    key_weight,
    value_weight,
    query,
    grad_context,
    target_segment,
    memory_segment,
    example_pack,
    example_slot,
):
    my_index = lax.axis_index("dp")
    width = key_weight.shape[1]
    stacked = jnp.concatenate((key_weight, value_weight), axis=1)
    weights = lax.all_gather(stacked, "dp", axis=0, tiled=True)
    my_packs = lax.dynamic_index_in_dim(example_pack, my_index, 0, keepdims=False)
    slots = target_slots(target_segment[0], my_packs)
    outgoing = pack_slots(slots, query, grad_context)
    arrived = lax.all_to_all(outgoing, "dp", split_axis=0, concat_axis=0, tiled=True)
    owned = example_pack == my_index
    wanted = jnp.where(
        jnp.any(owned, axis=1), jnp.sum(jnp.where(owned, example_slot, 0), axis=1), -1
    )
    kv = dot(memory, weights, 1, 0).astype(jnp.bfloat16)
    answers, grad_keys, grad_values = attend(wanted, memory_segment[0], arrived, kv)
    returned = lax.all_to_all(answers, "dp", split_axis=0, concat_axis=0, tiled=True)
    core = my_index % 2
    away = away_terms(relative_table(1 - core), memory, grad_keys, grad_values)
    other = lax.ppermute(away, "dp", shift(0, 0, 1))
    terms = memory_terms(grad_keys, grad_values, weights)
    other, terms = lax.optimization_barrier((other, terms))
    pieces = home_terms(relative_table(core), memory, grad_keys, grad_values, other)
    grad_memory = lax.psum_scatter(terms, "fsdp", scatter_dimension=0, tiled=True)
    context, grad_query = unpack_slots(slots, returned)
    sums_y = first_sums(ring_exchange(pieces[:RING], True))
    sums_x = first_sums(ring_exchange(pieces[RING:], False))
    weight_grads = jnp.concatenate(
        [
            sum_pieces(ring_exchange(sums_y, False)),
            sum_pieces(ring_exchange(sums_x, True)),
        ],
        axis=0,
    )
    return (
        context,
        grad_query,
        weight_grads[:, :width],
        weight_grads[:, width:],
        grad_memory,
    )


def solution(mesh):
    placed = (
        P("dp", None),
        P("dp", "fsdp"),
        P("dp", "fsdp"),
        P("dp", "fsdp"),
        P("dp", "fsdp"),
        P("dp", None),
        P("dp", None),
        P(),
        P(),
    )
    return jax.shard_map(
        per_device,
        mesh=mesh,
        in_specs=placed,
        out_specs=(
            P("dp", "fsdp"),
            P("dp", "fsdp"),
            P("dp", "fsdp"),
            P("dp", "fsdp"),
            P(("dp", "fsdp"), None),
        ),
        check_vma=False,
    )
```

```python
import jax
import jax.numpy as jnp
from jax import lax
from jax.experimental import pallas as pl
from jax.experimental.pallas import tpu as pltpu
from jax.sharding import PartitionSpec as P

HD = 256
PEERS = 32
DEPTH = 32
BLOCK_PEERS = 8
RING = 4


SCORE_SCALE = 0.0625
MASKED_SCORE = -1e30


def dot(left, right, left_dim, right_dim):
    return lax.dot_general(
        left, right, (((left_dim,), (right_dim,)), ((), ())), preferred_element_type=jnp.float32
    )


def target_slots(segment, my_packs):
    rows = segment.shape[0]
    earlier = jnp.sum((segment[None, :] < segment[:, None]).astype(jnp.int32), axis=1)
    example_ids = jnp.arange(my_packs.shape[0], dtype=jnp.int32)
    pack = jnp.sum(
        jnp.where(segment[:, None] == example_ids[None, :], my_packs[None, :], 0), axis=1
    )
    return pack * DEPTH + jnp.arange(rows, dtype=jnp.int32) - earlier


def pack_body(slot_ref, query_ref, grad_ref, out_ref):
    block = pl.program_id(0)
    rows = BLOCK_PEERS * DEPTH
    positions = block * rows + lax.broadcasted_iota(jnp.int32, (rows, slot_ref.shape[1]), 0)
    chosen = jnp.where(positions == slot_ref[...], 1.0, 0.0).astype(jnp.bfloat16)
    for part, source in enumerate((query_ref, grad_ref)):
        taken = dot(chosen, source[...], 1, 0).astype(jnp.bfloat16)
        out_ref[:, part] = taken.reshape(BLOCK_PEERS, DEPTH, taken.shape[1])


def pack_slots(slots, query, grad_context):
    rows, width = query.shape
    return pl.pallas_call(
        pack_body,
        grid=(PEERS // BLOCK_PEERS,),
        in_specs=[
            pl.BlockSpec((1, rows), lambda i: (0, 0)),
            pl.BlockSpec((rows, width), lambda i: (0, 0)),
            pl.BlockSpec((rows, width), lambda i: (0, 0)),
        ],
        out_specs=pl.BlockSpec((BLOCK_PEERS, 2, DEPTH, width), lambda i: (i, 0, 0, 0)),
        out_shape=jax.ShapeDtypeStruct((PEERS, 2, DEPTH, width), jnp.bfloat16),
        name="pack_slots",
    )(slots.reshape(1, rows), query, grad_context)


def unpack_body(slot_ref, in_ref, context_ref, grad_ref):
    slots = PEERS * DEPTH
    positions = lax.broadcasted_iota(jnp.int32, (slot_ref.shape[0], slots), 1)
    chosen = jnp.where(positions == slot_ref[...], 1.0, 0.0).astype(jnp.bfloat16)
    for part, target in enumerate((context_ref, grad_ref)):
        data = in_ref[:, part].reshape(slots, in_ref.shape[3])
        target[...] = dot(chosen, data, 1, 0).astype(jnp.bfloat16)


def unpack_slots(slots, returned):
    rows = slots.shape[0]
    width = returned.shape[3]
    half = width // 2
    return pl.pallas_call(
        unpack_body,
        grid=(2,),
        in_specs=[
            pl.BlockSpec((rows, 1), lambda i: (0, 0)),
            pl.BlockSpec((PEERS, 2, DEPTH, half), lambda i: (0, 0, 0, i)),
        ],
        out_specs=[
            pl.BlockSpec((rows, half), lambda i: (0, i)),
            pl.BlockSpec((rows, half), lambda i: (0, i)),
        ],
        out_shape=[jax.ShapeDtypeStruct((rows, width), jnp.bfloat16)] * 2,
        name="unpack_slots",
    )(slots.reshape(rows, 1), returned)


def attend_body(
    wanted_ref,
    segment_ref,
    in_ref,
    key_ref,
    value_ref,
    out_ref,
    grad_key_ref,
    grad_value_ref,
    key_sum,
    value_sum,
):
    block = pl.program_id(1)
    rows = BLOCK_PEERS * DEPTH
    query = in_ref[:, 0].reshape(rows, HD)
    grad = in_ref[:, 1].reshape(rows, HD)
    keys = key_ref[...]
    values = value_ref[...]
    valid = wanted_ref[...] == segment_ref[...]
    scores = jnp.where(valid, dot(query, keys, 1, 1) * SCORE_SCALE, MASKED_SCORE)
    grad_prob = dot(grad, values, 1, 1)
    raised = jnp.exp(scores - jnp.max(scores, axis=1, keepdims=True))
    probability = raised / jnp.sum(raised, axis=1, keepdims=True)
    rounded = probability.astype(jnp.bfloat16)
    row_delta = jnp.sum(probability * grad_prob, axis=1, keepdims=True)
    grad_scores = (probability * (grad_prob - row_delta) * SCORE_SCALE).astype(jnp.bfloat16)
    context = dot(rounded, values, 1, 0).astype(jnp.bfloat16)
    out_ref[:, 0] = context.reshape(BLOCK_PEERS, DEPTH, HD)
    grad_query = dot(grad_scores, keys, 1, 0).astype(jnp.bfloat16)
    out_ref[:, 1] = grad_query.reshape(BLOCK_PEERS, DEPTH, HD)
    key_term = dot(grad_scores, query, 0, 0)
    value_term = dot(rounded, grad, 0, 0)

    @pl.when(block == 0)
    def _():
        key_sum[...] = key_term
        value_sum[...] = value_term

    @pl.when(block > 0)
    def _():
        key_sum[...] += key_term
        value_sum[...] += value_term

    @pl.when(block == pl.num_programs(1) - 1)
    def _():
        grad_key_ref[...] = key_sum[...].astype(jnp.bfloat16)
        grad_value_ref[...] = value_sum[...].astype(jnp.bfloat16)


def attend(wanted, segment, arrived, kv):
    memory_rows = segment.shape[0]
    width = arrived.shape[3]
    heads = width // HD
    rows = BLOCK_PEERS * DEPTH
    wanted_rows = jnp.broadcast_to(wanted[:, None], (PEERS, DEPTH)).reshape(PEERS * DEPTH, 1)
    return pl.pallas_call(
        attend_body,
        grid=(heads, PEERS // BLOCK_PEERS),
        in_specs=[
            pl.BlockSpec((rows, 1), lambda h, i: (i, 0)),
            pl.BlockSpec((1, memory_rows), lambda h, i: (0, 0)),
            pl.BlockSpec((BLOCK_PEERS, 2, DEPTH, HD), lambda h, i: (i, 0, 0, h)),
            pl.BlockSpec((memory_rows, HD), lambda h, i: (0, h)),
            pl.BlockSpec((memory_rows, HD), lambda h, i: (0, heads + h)),
        ],
        out_specs=[
            pl.BlockSpec((BLOCK_PEERS, 2, DEPTH, HD), lambda h, i: (i, 0, 0, h)),
            pl.BlockSpec((memory_rows, HD), lambda h, i: (0, h)),
            pl.BlockSpec((memory_rows, HD), lambda h, i: (0, h)),
        ],
        out_shape=[
            jax.ShapeDtypeStruct(arrived.shape, jnp.bfloat16),
            jax.ShapeDtypeStruct((memory_rows, width), jnp.bfloat16),
            jax.ShapeDtypeStruct((memory_rows, width), jnp.bfloat16),
        ],
        scratch_shapes=[pltpu.VMEM((memory_rows, HD), jnp.float32)] * 2,
        name="attend",
    )(wanted_rows, segment.reshape(1, memory_rows), arrived, kv, kv)


def peer_of(y, x, core):
    return (y % RING) * 2 * RING + (x % RING) * 2 + core


def shift(y_step, x_step, swap):
    return [
        (peer_of(y, x, core), peer_of(y + y_step, x + x_step, core ^ swap))
        for y in range(RING)
        for x in range(RING)
        for core in range(2)
    ]


def relative_table(core):
    index = lax.axis_index("dp")
    steps = jnp.arange(RING * RING, dtype=jnp.int32)
    return peer_of(index // (2 * RING) + steps // RING, index // 2 % RING + steps % RING, core)


def joined_columns(refs):
    return jnp.concatenate([ref[...] for ref in refs], axis=1)


def column_specs(rows, block):
    return [
        pl.BlockSpec((rows, block), lambda i, table, j=j: (0, table[i * RING + j]))
        for j in range(RING)
    ]


def away_body(table_ref, *refs):
    del table_ref
    grad_key_ref, grad_value_ref, out_ref = refs[RING:]
    width = grad_key_ref.shape[1]
    columns = joined_columns(refs[:RING])
    out_ref[:, :width] = dot(columns, grad_key_ref[...], 0, 0).astype(jnp.bfloat16)
    out_ref[:, width:] = dot(columns, grad_value_ref[...], 0, 0).astype(jnp.bfloat16)


def away_terms(table, memory, grad_keys, grad_values):
    rows, model = memory.shape
    width = grad_keys.shape[1]
    block = model // PEERS
    return pl.pallas_call(
        away_body,
        grid_spec=pltpu.PrefetchScalarGridSpec(
            num_scalar_prefetch=1,
            grid=(RING,),
            in_specs=column_specs(rows, block)
            + [
                pl.BlockSpec((rows, width), lambda i, table: (0, 0)),
                pl.BlockSpec((rows, width), lambda i, table: (0, 0)),
            ],
            out_specs=pl.BlockSpec((RING * block, 2 * width), lambda i, table: (i, 0)),
        ),
        out_shape=jax.ShapeDtypeStruct((model // 2, 2 * width), jnp.bfloat16),
        name="away_terms",
    )(table, *([memory] * RING), grad_keys, grad_values)


def home_body(table_ref, *refs):
    del table_ref
    grad_key_ref, grad_value_ref, other_ref = refs[RING : RING + 3]
    out_refs = refs[RING + 3 :]
    y_step = pl.program_id(0)
    width = grad_key_ref.shape[1]
    half = out_refs[0].shape[1]
    columns = joined_columns(refs[:RING])
    for start, grad_ref in ((0, grad_key_ref), (width, grad_value_ref)):
        total = dot(columns, grad_ref[...], 0, 0)
        total += other_ref[:, start : start + width].astype(jnp.float32)
        total = total.astype(jnp.bfloat16).reshape(RING, 2 * half, width)
        for step in range(RING):
            out_refs[RING + step][y_step, :, start : start + width] = total[step, half:]

            @pl.when(y_step == step)
            def _():
                out_refs[step][:, :, start : start + width] = total[:, :half]


def home_terms(table, memory, grad_keys, grad_values, other):
    rows, model = memory.shape
    width = grad_keys.shape[1]
    block = model // PEERS
    piece = (RING, block // 2, 2 * width)
    return pl.pallas_call(
        home_body,
        grid_spec=pltpu.PrefetchScalarGridSpec(
            num_scalar_prefetch=1,
            grid=(RING,),
            in_specs=column_specs(rows, block)
            + [
                pl.BlockSpec((rows, width), lambda i, table: (0, 0)),
                pl.BlockSpec((rows, width), lambda i, table: (0, 0)),
                pl.BlockSpec((RING * block, 2 * width), lambda i, table: (i, 0)),
            ],
            out_specs=[pl.BlockSpec(piece, lambda i, table: (0, 0, 0))] * (2 * RING),
        ),
        out_shape=[jax.ShapeDtypeStruct(piece, jnp.bfloat16)] * (2 * RING),
        name="home_terms",
    )(table, *([memory] * RING), grad_keys, grad_values, other)


def sum_pieces(pieces):
    total = pieces[0].astype(jnp.float32)
    for piece in pieces[1:]:
        total += piece.astype(jnp.float32)
    return total


def ring_exchange(pieces, along_y):
    received = [pieces[0]]
    for step in range(1, RING):
        perm = shift(step, 0, 0) if along_y else shift(0, step, 0)
        received.append(lax.ppermute(pieces[step], "dp", perm))
    return received


def first_sums(received):
    return [
        sum_pieces([piece[step] for piece in received]).astype(jnp.bfloat16)
        for step in range(RING)
    ]


def memory_body(grad_key_ref, grad_value_ref, weight_ref, out_ref):
    width = grad_key_ref.shape[1]
    total = dot(grad_key_ref[...], weight_ref[:, :width], 1, 1)
    total += dot(grad_value_ref[...], weight_ref[:, width:], 1, 1)
    out_ref[...] = total.astype(jnp.bfloat16)


def memory_terms(grad_keys, grad_values, weights):
    rows, width = grad_keys.shape
    model = weights.shape[0]
    block = 512
    return pl.pallas_call(
        memory_body,
        grid=(model // block,),
        in_specs=[
            pl.BlockSpec((rows, width), lambda i: (0, 0)),
            pl.BlockSpec((rows, width), lambda i: (0, 0)),
            pl.BlockSpec((block, 2 * width), lambda i: (i, 0)),
        ],
        out_specs=pl.BlockSpec((rows, block), lambda i: (0, i)),
        out_shape=jax.ShapeDtypeStruct((rows, model), jnp.bfloat16),
        name="memory_terms",
    )(grad_keys, grad_values, weights)


def per_device(
    memory,
    key_weight,
    value_weight,
    query,
    grad_context,
    target_segment,
    memory_segment,
    example_pack,
    example_slot,
):
    my_index = lax.axis_index("dp")
    width = key_weight.shape[1]
    stacked = jnp.concatenate((key_weight, value_weight), axis=1)
    weights = lax.all_gather(stacked, "dp", axis=0, tiled=True)
    my_packs = lax.dynamic_index_in_dim(example_pack, my_index, 0, keepdims=False)
    slots = target_slots(target_segment[0], my_packs)
    outgoing = pack_slots(slots, query, grad_context)
    arrived = lax.all_to_all(outgoing, "dp", split_axis=0, concat_axis=0, tiled=True)
    owned = example_pack == my_index
    wanted = jnp.where(
        jnp.any(owned, axis=1), jnp.sum(jnp.where(owned, example_slot, 0), axis=1), -1
    )
    kv = dot(memory, weights, 1, 0).astype(jnp.bfloat16)
    answers, grad_keys, grad_values = attend(wanted, memory_segment[0], arrived, kv)
    returned = lax.all_to_all(answers, "dp", split_axis=0, concat_axis=0, tiled=True)
    core = my_index % 2
    away = away_terms(relative_table(1 - core), memory, grad_keys, grad_values)
    other = lax.ppermute(away, "dp", shift(0, 0, 1))
    terms = memory_terms(grad_keys, grad_values, weights)
    other, terms, returned = lax.optimization_barrier((other, terms, returned))
    pieces = home_terms(relative_table(core), memory, grad_keys, grad_values, other)
    grad_memory = lax.psum_scatter(terms, "fsdp", scatter_dimension=0, tiled=True)
    context, grad_query = unpack_slots(slots, returned)
    sums_y = first_sums(ring_exchange(pieces[:RING], True))
    sums_x = first_sums(ring_exchange(pieces[RING:], False))
    weight_grads = jnp.concatenate(
        [
            sum_pieces(ring_exchange(sums_y, False)),
            sum_pieces(ring_exchange(sums_x, True)),
        ],
        axis=0,
    )
    return (
        context,
        grad_query,
        weight_grads[:, :width],
        weight_grads[:, width:],
        grad_memory,
    )


def solution(mesh):
    placed = (
        P("dp", None),
        P("dp", "fsdp"),
        P("dp", "fsdp"),
        P("dp", "fsdp"),
        P("dp", "fsdp"),
        P("dp", None),
        P("dp", None),
        P(),
        P(),
    )
    return jax.shard_map(
        per_device,
        mesh=mesh,
        in_specs=placed,
        out_specs=(
            P("dp", "fsdp"),
            P("dp", "fsdp"),
            P("dp", "fsdp"),
            P("dp", "fsdp"),
            P(("dp", "fsdp"), None),
        ),
        check_vma=False,
    )
```

```python
import jax
import jax.numpy as jnp
from jax import lax
from jax.experimental import pallas as pl
from jax.experimental.pallas import tpu as pltpu
from jax.sharding import PartitionSpec as P

HD = 256
PEERS = 32
DEPTH = 32
BLOCK_PEERS = 8
RING = 4


SCORE_SCALE = 0.0625
MASKED_SCORE = -1e30


def dot(left, right, left_dim, right_dim):
    return lax.dot_general(
        left, right, (((left_dim,), (right_dim,)), ((), ())), preferred_element_type=jnp.float32
    )


def target_slots(segment, my_packs):
    rows = segment.shape[0]
    earlier = jnp.sum((segment[None, :] < segment[:, None]).astype(jnp.int32), axis=1)
    example_ids = jnp.arange(my_packs.shape[0], dtype=jnp.int32)
    pack = jnp.sum(
        jnp.where(segment[:, None] == example_ids[None, :], my_packs[None, :], 0), axis=1
    )
    return pack * DEPTH + jnp.arange(rows, dtype=jnp.int32) - earlier


def pack_body(slot_ref, query_ref, grad_ref, out_ref):
    block = pl.program_id(0)
    rows = BLOCK_PEERS * DEPTH
    positions = block * rows + lax.broadcasted_iota(jnp.int32, (rows, slot_ref.shape[1]), 0)
    chosen = jnp.where(positions == slot_ref[...], 1.0, 0.0).astype(jnp.bfloat16)
    for part, source in enumerate((query_ref, grad_ref)):
        taken = dot(chosen, source[...], 1, 0).astype(jnp.bfloat16)
        out_ref[:, part] = taken.reshape(BLOCK_PEERS, DEPTH, taken.shape[1])


def pack_slots(slots, query, grad_context):
    rows, width = query.shape
    return pl.pallas_call(
        pack_body,
        grid=(PEERS // BLOCK_PEERS,),
        in_specs=[
            pl.BlockSpec((1, rows), lambda i: (0, 0)),
            pl.BlockSpec((rows, width), lambda i: (0, 0)),
            pl.BlockSpec((rows, width), lambda i: (0, 0)),
        ],
        out_specs=pl.BlockSpec((BLOCK_PEERS, 2, DEPTH, width), lambda i: (i, 0, 0, 0)),
        out_shape=jax.ShapeDtypeStruct((PEERS, 2, DEPTH, width), jnp.bfloat16),
        name="pack_slots",
    )(slots.reshape(1, rows), query, grad_context)


def unpack_body(slot_ref, in_ref, context_ref, grad_ref):
    slots = PEERS * DEPTH
    positions = lax.broadcasted_iota(jnp.int32, (slot_ref.shape[0], slots), 1)
    chosen = jnp.where(positions == slot_ref[...], 1.0, 0.0).astype(jnp.bfloat16)
    for part, target in enumerate((context_ref, grad_ref)):
        data = in_ref[:, part].reshape(slots, in_ref.shape[3])
        target[...] = dot(chosen, data, 1, 0).astype(jnp.bfloat16)


def unpack_slots(slots, returned):
    rows = slots.shape[0]
    width = returned.shape[3]
    half = width // 2
    return pl.pallas_call(
        unpack_body,
        grid=(2,),
        in_specs=[
            pl.BlockSpec((rows, 1), lambda i: (0, 0)),
            pl.BlockSpec((PEERS, 2, DEPTH, half), lambda i: (0, 0, 0, i)),
        ],
        out_specs=[
            pl.BlockSpec((rows, half), lambda i: (0, i)),
            pl.BlockSpec((rows, half), lambda i: (0, i)),
        ],
        out_shape=[jax.ShapeDtypeStruct((rows, width), jnp.bfloat16)] * 2,
        name="unpack_slots",
    )(slots.reshape(rows, 1), returned)


def attend_body(
    wanted_ref,
    segment_ref,
    in_ref,
    key_ref,
    value_ref,
    out_ref,
    grad_key_ref,
    grad_value_ref,
    key_sum,
    value_sum,
):
    block = pl.program_id(1)
    rows = BLOCK_PEERS * DEPTH
    query = in_ref[:, 0].reshape(rows, HD)
    grad = in_ref[:, 1].reshape(rows, HD)
    keys = key_ref[...]
    values = value_ref[...]
    valid = wanted_ref[...] == segment_ref[...]
    scores = jnp.where(valid, dot(query, keys, 1, 1) * SCORE_SCALE, MASKED_SCORE)
    grad_prob = dot(grad, values, 1, 1)
    raised = jnp.exp(scores - jnp.max(scores, axis=1, keepdims=True))
    probability = raised / jnp.sum(raised, axis=1, keepdims=True)
    rounded = probability.astype(jnp.bfloat16)
    row_delta = jnp.sum(probability * grad_prob, axis=1, keepdims=True)
    grad_scores = (probability * (grad_prob - row_delta) * SCORE_SCALE).astype(jnp.bfloat16)
    context = dot(rounded, values, 1, 0).astype(jnp.bfloat16)
    out_ref[:, 0] = context.reshape(BLOCK_PEERS, DEPTH, HD)
    grad_query = dot(grad_scores, keys, 1, 0).astype(jnp.bfloat16)
    out_ref[:, 1] = grad_query.reshape(BLOCK_PEERS, DEPTH, HD)
    key_term = dot(grad_scores, query, 0, 0)
    value_term = dot(rounded, grad, 0, 0)

    @pl.when(block == 0)
    def _():
        key_sum[...] = key_term
        value_sum[...] = value_term

    @pl.when(block > 0)
    def _():
        key_sum[...] += key_term
        value_sum[...] += value_term

    @pl.when(block == pl.num_programs(1) - 1)
    def _():
        grad_key_ref[...] = key_sum[...].astype(jnp.bfloat16)
        grad_value_ref[...] = value_sum[...].astype(jnp.bfloat16)


def attend(wanted, segment, arrived, kv):
    memory_rows = segment.shape[0]
    width = arrived.shape[3]
    heads = width // HD
    rows = BLOCK_PEERS * DEPTH
    wanted_rows = jnp.broadcast_to(wanted[:, None], (PEERS, DEPTH)).reshape(PEERS * DEPTH, 1)
    return pl.pallas_call(
        attend_body,
        grid=(heads, PEERS // BLOCK_PEERS),
        in_specs=[
            pl.BlockSpec((rows, 1), lambda h, i: (i, 0)),
            pl.BlockSpec((1, memory_rows), lambda h, i: (0, 0)),
            pl.BlockSpec((BLOCK_PEERS, 2, DEPTH, HD), lambda h, i: (i, 0, 0, h)),
            pl.BlockSpec((memory_rows, HD), lambda h, i: (0, h)),
            pl.BlockSpec((memory_rows, HD), lambda h, i: (0, heads + h)),
        ],
        out_specs=[
            pl.BlockSpec((BLOCK_PEERS, 2, DEPTH, HD), lambda h, i: (i, 0, 0, h)),
            pl.BlockSpec((memory_rows, HD), lambda h, i: (0, h)),
            pl.BlockSpec((memory_rows, HD), lambda h, i: (0, h)),
        ],
        out_shape=[
            jax.ShapeDtypeStruct(arrived.shape, jnp.bfloat16),
            jax.ShapeDtypeStruct((memory_rows, width), jnp.bfloat16),
            jax.ShapeDtypeStruct((memory_rows, width), jnp.bfloat16),
        ],
        scratch_shapes=[pltpu.VMEM((memory_rows, HD), jnp.float32)] * 2,
        name="attend",
    )(wanted_rows, segment.reshape(1, memory_rows), arrived, kv, kv)


def peer_of(y, x, core):
    return (y % RING) * 2 * RING + (x % RING) * 2 + core


def shift(y_step, x_step, swap):
    return [
        (peer_of(y, x, core), peer_of(y + y_step, x + x_step, core ^ swap))
        for y in range(RING)
        for x in range(RING)
        for core in range(2)
    ]


def relative_table(core):
    index = lax.axis_index("dp")
    steps = jnp.arange(RING * RING, dtype=jnp.int32)
    return peer_of(index // (2 * RING) + steps // RING, index // 2 % RING + steps % RING, core)


def joined_columns(refs):
    return jnp.concatenate([ref[...] for ref in refs], axis=1)


def column_specs(rows, block):
    return [
        pl.BlockSpec((rows, block), lambda i, table, j=j: (0, table[i * RING + j]))
        for j in range(RING)
    ]


def away_body(table_ref, *refs):
    del table_ref
    grad_key_ref, grad_value_ref, out_ref = refs[RING:]
    width = grad_key_ref.shape[1]
    columns = joined_columns(refs[:RING])
    out_ref[:, :width] = dot(columns, grad_key_ref[...], 0, 0).astype(jnp.bfloat16)
    out_ref[:, width:] = dot(columns, grad_value_ref[...], 0, 0).astype(jnp.bfloat16)


def away_terms(table, memory, grad_keys, grad_values):
    rows, model = memory.shape
    width = grad_keys.shape[1]
    block = model // PEERS
    return pl.pallas_call(
        away_body,
        grid_spec=pltpu.PrefetchScalarGridSpec(
            num_scalar_prefetch=1,
            grid=(RING,),
            in_specs=column_specs(rows, block)
            + [
                pl.BlockSpec((rows, width), lambda i, table: (0, 0)),
                pl.BlockSpec((rows, width), lambda i, table: (0, 0)),
            ],
            out_specs=pl.BlockSpec((RING * block, 2 * width), lambda i, table: (i, 0)),
        ),
        out_shape=jax.ShapeDtypeStruct((model // 2, 2 * width), jnp.bfloat16),
        name="away_terms",
    )(table, *([memory] * RING), grad_keys, grad_values)


def home_body(table_ref, *refs):
    del table_ref
    grad_key_ref, grad_value_ref, other_ref = refs[RING : RING + 3]
    out_refs = refs[RING + 3 :]
    y_step = pl.program_id(0)
    width = grad_key_ref.shape[1]
    half = out_refs[0].shape[1]
    columns = joined_columns(refs[:RING])
    for start, grad_ref in ((0, grad_key_ref), (width, grad_value_ref)):
        total = dot(columns, grad_ref[...], 0, 0)
        total += other_ref[:, start : start + width].astype(jnp.float32)
        total = total.astype(jnp.bfloat16).reshape(RING, 2 * half, width)
        for step in range(RING):
            out_refs[RING + step][y_step, :, start : start + width] = total[step, half:]

            @pl.when(y_step == step)
            def _():
                out_refs[step][:, :, start : start + width] = total[:, :half]


def home_terms(table, memory, grad_keys, grad_values, other):
    rows, model = memory.shape
    width = grad_keys.shape[1]
    block = model // PEERS
    piece = (RING, block // 2, 2 * width)
    return pl.pallas_call(
        home_body,
        grid_spec=pltpu.PrefetchScalarGridSpec(
            num_scalar_prefetch=1,
            grid=(RING,),
            in_specs=column_specs(rows, block)
            + [
                pl.BlockSpec((rows, width), lambda i, table: (0, 0)),
                pl.BlockSpec((rows, width), lambda i, table: (0, 0)),
                pl.BlockSpec((RING * block, 2 * width), lambda i, table: (i, 0)),
            ],
            out_specs=[pl.BlockSpec(piece, lambda i, table: (0, 0, 0))] * (2 * RING),
        ),
        out_shape=[jax.ShapeDtypeStruct(piece, jnp.bfloat16)] * (2 * RING),
        name="home_terms",
    )(table, *([memory] * RING), grad_keys, grad_values, other)


def sum_pieces(pieces):
    total = pieces[0].astype(jnp.float32)
    for piece in pieces[1:]:
        total += piece.astype(jnp.float32)
    return total


def ring_exchange(pieces, along_y):
    received = [pieces[0]]
    for step in range(1, RING):
        perm = shift(step, 0, 0) if along_y else shift(0, step, 0)
        received.append(lax.ppermute(pieces[step], "dp", perm))
    return received


def first_sums(received):
    return [
        sum_pieces([piece[step] for piece in received]).astype(jnp.bfloat16)
        for step in range(RING)
    ]


def memory_body(grad_key_ref, grad_value_ref, weight_ref, out_ref):
    width = grad_key_ref.shape[1]
    total = dot(grad_key_ref[...], weight_ref[:, :width], 1, 1)
    total += dot(grad_value_ref[...], weight_ref[:, width:], 1, 1)
    out_ref[...] = total.astype(jnp.bfloat16)


def memory_terms(grad_keys, grad_values, weights):
    rows, width = grad_keys.shape
    model = weights.shape[0]
    block = 512
    return pl.pallas_call(
        memory_body,
        grid=(model // block,),
        in_specs=[
            pl.BlockSpec((rows, width), lambda i: (0, 0)),
            pl.BlockSpec((rows, width), lambda i: (0, 0)),
            pl.BlockSpec((block, 2 * width), lambda i: (i, 0)),
        ],
        out_specs=pl.BlockSpec((rows, block), lambda i: (0, i)),
        out_shape=jax.ShapeDtypeStruct((rows, model), jnp.bfloat16),
        name="memory_terms",
    )(grad_keys, grad_values, weights)


def per_device(
    memory,
    key_weight,
    value_weight,
    query,
    grad_context,
    target_segment,
    memory_segment,
    example_pack,
    example_slot,
):
    my_index = lax.axis_index("dp")
    width = key_weight.shape[1]
    stacked = jnp.concatenate((key_weight, value_weight), axis=1)
    weights = lax.all_gather(stacked, "dp", axis=0, tiled=True)
    my_packs = lax.dynamic_index_in_dim(example_pack, my_index, 0, keepdims=False)
    slots = target_slots(target_segment[0], my_packs)
    outgoing = pack_slots(slots, query, grad_context)
    arrived = lax.all_to_all(outgoing, "dp", split_axis=0, concat_axis=0, tiled=True)
    owned = example_pack == my_index
    wanted = jnp.where(
        jnp.any(owned, axis=1), jnp.sum(jnp.where(owned, example_slot, 0), axis=1), -1
    )
    kv = dot(memory, weights, 1, 0).astype(jnp.bfloat16)
    answers, grad_keys, grad_values = attend(wanted, memory_segment[0], arrived, kv)
    returned = lax.all_to_all(answers, "dp", split_axis=0, concat_axis=0, tiled=True)
    core = my_index % 2
    away = away_terms(relative_table(1 - core), memory, grad_keys, grad_values)
    other = lax.ppermute(away, "dp", shift(0, 0, 1))
    terms = memory_terms(grad_keys, grad_values, weights)
    other, terms = lax.optimization_barrier((other, terms))
    pieces = home_terms(relative_table(core), memory, grad_keys, grad_values, other)
    terms, returned, pieces = lax.optimization_barrier((terms, returned, pieces))
    grad_memory = lax.psum_scatter(terms, "fsdp", scatter_dimension=0, tiled=True)
    context, grad_query = unpack_slots(slots, returned)
    sums_y = first_sums(ring_exchange(pieces[:RING], True))
    sums_x = first_sums(ring_exchange(pieces[RING:], False))
    weight_grads = jnp.concatenate(
        [
            sum_pieces(ring_exchange(sums_y, False)),
            sum_pieces(ring_exchange(sums_x, True)),
        ],
        axis=0,
    )
    return (
        context,
        grad_query,
        weight_grads[:, :width],
        weight_grads[:, width:],
        grad_memory,
    )


def solution(mesh):
    placed = (
        P("dp", None),
        P("dp", "fsdp"),
        P("dp", "fsdp"),
        P("dp", "fsdp"),
        P("dp", "fsdp"),
        P("dp", None),
        P("dp", None),
        P(),
        P(),
    )
    return jax.shard_map(
        per_device,
        mesh=mesh,
        in_specs=placed,
        out_specs=(
            P("dp", "fsdp"),
            P("dp", "fsdp"),
            P("dp", "fsdp"),
            P("dp", "fsdp"),
            P(("dp", "fsdp"), None),
        ),
        check_vma=False,
    )
```
